32 devices in a mesh: seq: 2 (over core), expert: 16 (over z, y, x).
Axes of the slice: x: 2, y: 2, z: 4, core: 2. Of those that a mesh axis runs over, the one named last changes fastest.
Arguments:
- tokens: bfloat16 [4096, 4096], P(('seq', 'expert')), may hold values from -6 to 6
- routes: int32 [4096, 2], P(('seq', 'expert')), may hold values from 0 to 15, all different within a row; in each aligned block of 128 rows (0 to 127, 128 to 255, ...) at most 24 rows name the same one
- route_probs: float32 [4096, 2], P(('seq', 'expert')), may hold values from 0.25 to 1
- gate_weight: bfloat16 [16, 4096, 768], P('expert', None, 'seq'), may hold values from -0.09375 to 0.09375
- up_weight: bfloat16 [16, 4096, 768], P('expert', None, 'seq'), may hold values from -0.09375 to 0.09375
- down_weight: bfloat16 [16, 768, 4096], P('expert', 'seq'), may hold values from -0.21875 to 0.21875
- grad_out: bfloat16 [4096, 4096], P(('seq', 'expert')), may hold values from -3 to 3
Outputs:
- grad_tokens: bfloat16 [4096, 4096], P(('seq', 'expert'))
- grad_probs: bfloat16 [4096, 2], P(('seq', 'expert'))
The draws below stay inside these ranges and needn't reach their ends.
Inputs may be any that keep to these rules, and one draw needn't show every extreme that they name: `routes`: each token names 2 different experts. Among the tokens of one device no expert is named by more than 24 tokens, and in every draw some device names some expert exactly 24 times.
All inputs are finite; a program needn't handle non-finite values.
Results may differ from the reference program's by a relative error of at most 0.01.
Values may be sent and summed in bfloat16 or wider, within the bound.
A program may use at most 128 MiB of HBM per device.

```python
import math
import jax
import jax.numpy as jnp
import numpy as np
from jax import lax

D = 4096
H = 768
TOPK = 2
TOK_DEV = 128
EXPERTS = 16
CAP = 24
TOKENS = 4096
N_SEQ = 2
N_EXPERT = 16


def block_levels(stream_key, shape, split, least, top_value):
    loudness = 1.0
    for position, blocks in split:
        draws = jax.random.uniform(jax.random.fold_in(jax.random.fold_in(stream_key, 6), position), (blocks,), jnp.float32, least / len(split), top_value / len(split))
        loudness = loudness * jnp.repeat(jnp.exp(draws), shape[position] // blocks).reshape((-1,) + (1,) * (len(shape) - 1 - position))
    return loudness


def shared_out(stream_key, own, number, rows, number_of, top, reach, slope):
    sequence = jax.random.permutation(stream_key, number_of)
    packed, usual = load_shares(number_of, rows * top, reach, slope, True), load_shares(number_of, rows * top, reach, slope, False)
    places = jnp.arange(number_of)

    def named(lengths, rotation):
        used = int((lengths > 0).sum())
        fixed = max(1, used // 4)
        moved = fixed + (places - fixed + rotation * (used - fixed)) % max(1, number_of - fixed)
        return jnp.zeros((number_of,), jnp.int32).at[sequence[jnp.where(places < fixed, places, moved)]].set(jnp.asarray(lengths, jnp.int32))

    lengths = jnp.where(number % 4 == 0, named(packed, number // 4), named(usual, number - number // 4 - 1))
    mixed = jax.random.permutation(jax.random.fold_in(own, 3), number_of)
    donor, sink = mixed[0:number_of // 2 * 2:2], mixed[1:number_of // 2 * 2:2]
    margin = jnp.minimum(lengths[donor] - 1, reach - lengths[sink]) // 2
    margin = jnp.where((donor == sequence[0]) | (sink == sequence[0]) | (lengths[sink] == 0), 0, jnp.maximum(margin, 0))
    moved = jax.random.randint(jax.random.fold_in(own, 4), (number_of // 2,), 0, 1 << 20) % (margin + 1)
    lengths = lengths.at[donor].add(-moved).at[sink].add(moved)
    members = jnp.searchsorted(jnp.cumsum(lengths), jnp.arange(rows * top), side="right").astype(jnp.int32)
    grid = members.reshape(top, rows).T
    grid = grid[jax.random.permutation(jax.random.fold_in(own, 1), rows)]
    rotation = jax.random.randint(jax.random.fold_in(own, 2), (rows, 1), 0, top)
    return jnp.take_along_axis(grid, (jnp.arange(top)[None, :] + rotation) % top, axis=1)


def load_shares(amount, total, limit, slope, full):
    weights = [(1 << 20) // math.isqrt(standing ** slope) + 1 for standing in range(1, amount + 1)]
    largest = limit if full else min(limit, max(-(-total // amount), total * weights[0] // sum(weights)))
    least = 1 if total - largest >= amount - 1 else 0
    given, surplus = [largest] + [least] * (amount - 1), total - largest - least * (amount - 1)
    while surplus > 0:
        free = [i for i in range(1, amount) if given[i] < largest] or [i for i in range(1, amount) if given[i] < limit]
        mass, remaining = sum([weights[i] for i in free]), surplus
        for i in free:
            more = min(limit - given[i], max(1, remaining * weights[i] // mass), surplus)
            given[i] = given[i] + more
            surplus = surplus - more
    return np.array(given)


def gaussian(rng, extent, scale, bound, split=(), kind=jnp.bfloat16):
    entries = scale * jax.random.normal(rng, extent, jnp.float32)
    if split:
        entries = entries * block_levels(rng, extent, split, -0.22, 0.18)
    return jnp.clip(entries, -bound, bound).astype(kind)


def setup_inputs(seed: int = 0) -> dict:
    key_of = jax.random.split(jax.random.key(seed), 8)
    tokens = gaussian(key_of[0], (TOKENS, D), 1.0, 6.0, ((0, 32),))
    routes_keys = jax.random.split(jax.random.fold_in(key_of[1], 1), TOKENS // TOK_DEV)
    routes_turns = jax.random.permutation(jax.random.fold_in(key_of[1], 3), TOKENS // TOK_DEV)
    routes = jax.vmap(lambda own, number: shared_out(jax.random.fold_in(key_of[1], 2), own, number, TOK_DEV, EXPERTS, TOPK, CAP, 1))(routes_keys, routes_turns).reshape((TOKENS, TOPK))
    route_probs = jnp.clip(0.25 + 0.75 * jax.random.uniform(key_of[2], (TOKENS, TOPK), jnp.float32) ** block_levels(key_of[2], (TOKENS, TOPK), ((0, 32),), -0.2, 0.2), 0.25, 1.0)
    gate_weight = gaussian(key_of[3], (EXPERTS, D, H), D ** -0.5, 0.09375, ((0, 16), (2, 2)))
    up_weight = gaussian(key_of[4], (EXPERTS, D, H), D ** -0.5, 0.09375, ((0, 16), (2, 2)))
    down_weight = gaussian(key_of[5], (EXPERTS, H, D), H ** -0.5, 0.21875, ((0, 16), (1, 2)))
    grad_out = gaussian(key_of[6], (TOKENS, D), 0.5, 3.0, ((0, 32),))
    return dict(tokens=tokens, routes=routes, route_probs=route_probs, gate_weight=gate_weight, up_weight=up_weight, down_weight=down_weight, grad_out=grad_out)


def expert_terms(rows_in, rows_grad, gate_w, up_w, down_w):
    contract = (((1,), (1,)), ((), ()))
    gating = jnp.dot(rows_in, gate_w, preferred_element_type=jnp.float32)
    lifted = jnp.dot(rows_in, up_w, preferred_element_type=jnp.float32)
    sigmoid = jax.nn.sigmoid(gating)
    active = gating * sigmoid
    hidden = (active * lifted).astype(jnp.bfloat16)
    grad_hidden = lax.dot_general(rows_grad, down_w, contract, preferred_element_type=jnp.float32)
    grad_prob = jnp.sum(hidden.astype(jnp.float32) * grad_hidden, axis=1)
    slope_term = sigmoid * (1.0 + gating * (1.0 - sigmoid))
    grad_gate = (grad_hidden * lifted * slope_term).astype(jnp.bfloat16)
    grad_up = (grad_hidden * active).astype(jnp.bfloat16)
    grad_rows = lax.dot_general(grad_gate, gate_w, contract, preferred_element_type=jnp.float32)
    grad_rows = grad_rows + lax.dot_general(grad_up, up_w, contract, preferred_element_type=jnp.float32)
    return grad_rows, grad_prob


def reference(tokens, routes, route_probs, gate_weight, up_weight, down_weight, grad_out):
    total = TOKENS * TOPK
    chosen = routes.reshape(-1).astype(jnp.int32)
    ordering = jnp.argsort(chosen, stable=True).astype(jnp.int32)
    counts = jnp.zeros((EXPERTS,), jnp.int32).at[chosen].add(1)
    offsets = (jnp.cumsum(counts) - counts).astype(jnp.int32)
    row_limit = CAP * N_EXPERT * N_SEQ
    flat_probs = route_probs.reshape(-1)

    def per_expert(totals, expert):
        grad_acc, prob_acc = totals
        lanes = jnp.arange(row_limit, dtype=jnp.int32)
        flat_index = jnp.clip(offsets[expert] + lanes, 0, total - 1).astype(jnp.int32)
        is_live = lanes < counts[expert]
        assigned = ordering[flat_index]
        source = (assigned // TOPK).astype(jnp.int32)
        grad_rows, grad_prob = expert_terms(tokens[source], grad_out[source], gate_weight[expert], up_weight[expert], down_weight[expert])
        grad_rows = lax.optimization_barrier(grad_rows.astype(jnp.bfloat16))
        grad_prob = lax.optimization_barrier(grad_prob.astype(jnp.bfloat16))
        weighting = jnp.where(is_live, flat_probs[assigned], 0.0).astype(jnp.float32)
        grad_acc = grad_acc.at[source].add(weighting[:, None] * grad_rows.astype(jnp.float32))
        prob_acc = prob_acc.at[assigned].add(jnp.where(is_live, grad_prob.astype(jnp.float32), 0.0))
        return (grad_acc, prob_acc), None

    start = (jnp.zeros((TOKENS, D), jnp.float32), jnp.zeros((total,), jnp.float32))
    (grad_acc, prob_acc), _ = lax.scan(per_expert, start, jnp.arange(EXPERTS, dtype=jnp.int32))
    return grad_acc.astype(jnp.bfloat16), prob_acc.reshape(TOKENS, TOPK).astype(jnp.bfloat16)
```

```python
import jax
import jax.numpy as jnp
from jax import lax
from jax.sharding import PartitionSpec as P

CHUNKS = 2
NT = (((1,), (1,)), ((), ()))


def dot(a, b):
    return jnp.dot(a, b, preferred_element_type=jnp.float32)


def dot_nt(a, b):
    return lax.dot_general(a, b, NT, preferred_element_type=jnp.float32)


def slots_of(routes, base, half, capacity):
    local = routes - base
    chosen = local.reshape(-1)
    onehot = (chosen[:, None] == jnp.arange(half, dtype=jnp.int32)[None, :]).astype(jnp.int32)
    before = jnp.cumsum(onehot, axis=0) - onehot
    position = jnp.sum(before * onehot, axis=1).reshape(routes.shape)
    valid = (local >= 0) & (local < half)
    return jnp.where(valid, local * capacity + position, -1)


def dispatch_of(slots, count):
    lanes = jnp.arange(count, dtype=jnp.int32)[:, None, None]
    return jnp.any(lanes == slots[None], axis=2).astype(jnp.bfloat16)


def weighting_of(slots, probs, count):
    lanes = jnp.arange(count, dtype=jnp.int32)[None, None, :]
    full = jnp.sum(jnp.where(slots[:, :, None] == lanes, probs[:, :, None], 0.0), axis=1)
    high = lax.reduce_precision(full, 8, 7)
    return high.astype(jnp.bfloat16), (full - high).astype(jnp.bfloat16)


def combine(weighting, rows):
    return dot(weighting[0], rows) + dot(weighting[1], rows)


def pick(slots, values):
    lanes = jnp.arange(values.shape[0], dtype=jnp.int32)[None, None, :]
    return jnp.sum(jnp.where(slots[:, :, None] == lanes, values[None, None, :], 0.0), axis=2)


def front(rows_in, gates, ups):
    return [(dot(rows_in, g), dot(rows_in, u)) for g, u in zip(gates, ups)]


def middle(terms, rows_grad, downs):
    prob, grads = 0.0, []
    for (gating, lifted), d in zip(terms, downs):
        sigmoid = jax.nn.sigmoid(gating)
        active = gating * sigmoid
        hidden = (active * lifted).astype(jnp.bfloat16)
        grad_hidden = dot_nt(rows_grad, d)
        prob = prob + jnp.sum(hidden.astype(jnp.float32) * grad_hidden, axis=1)
        slope_term = sigmoid * (1.0 + gating * (1.0 - sigmoid))
        grads.append(
            (
                (grad_hidden * lifted * slope_term).astype(jnp.bfloat16),
                (grad_hidden * active).astype(jnp.bfloat16),
            )
        )
    return grads, prob


def back(grads, gates, ups, columns):
    total = 0.0
    for (gg, gu), g, u in zip(grads, gates, ups):
        total = total + dot_nt(gg, g[columns]) + dot_nt(gu, u[columns])
    return total.astype(jnp.bfloat16)


def on_device(tokens, routes, route_probs, gate_weight, up_weight, down_weight, grad_out):
    tok_count, width = tokens.shape
    top_count = routes.shape[1]
    experts = lax.axis_size("expert")
    parts = lax.axis_size("seq")
    capacity = 3 * tok_count * top_count // (2 * experts)
    half = experts // 2
    count = half * capacity
    base = (lax.axis_index("expert") // half) * half
    swap = [(i, (i + half) % experts) for i in range(experts)]
    groups = [list(range(half)), list(range(half, experts))]

    def across(value):
        return lax.ppermute(value, "expert", swap)

    def exchange(value):
        value = value.reshape(half, capacity, -1)
        value = lax.all_to_all(
            value, "expert", split_axis=0, concat_axis=0, tiled=True, axis_index_groups=groups
        )
        return value.reshape(count, -1)

    far_routes, far_probs = across(routes), across(route_probs)
    far_tokens, far_grad = across(tokens), across(grad_out)

    gates, ups, downs = [gate_weight[0]], [up_weight[0]], [down_weight[0]]
    for shift in range(1, parts):
        turn = [(i, (i + shift) % parts) for i in range(parts)]
        gates.append(lax.ppermute(gate_weight[0], "seq", turn))
        ups.append(lax.ppermute(up_weight[0], "seq", turn))
        downs.append(lax.ppermute(down_weight[0], "seq", turn))

    near_slots = slots_of(routes, base, half, capacity)
    near_pick = dispatch_of(near_slots, count)
    near_in = exchange(dot(near_pick, tokens).astype(jnp.bfloat16))
    near_out = exchange(dot(near_pick, grad_out).astype(jnp.bfloat16))
    near_grads, near_prob = middle(front(near_in, gates, ups), near_out, downs)

    far_slots = slots_of(far_routes, base, half, capacity)
    far_pick = dispatch_of(far_slots, count)
    far_in = exchange(dot(far_pick, far_tokens).astype(jnp.bfloat16))
    far_terms = front(far_in, gates, ups)
    far_out = exchange(dot(far_pick, far_grad).astype(jnp.bfloat16))
    far_grads, far_prob = middle(far_terms, far_out, downs)

    near_weighting = weighting_of(near_slots, route_probs, count)
    far_weighting = weighting_of(far_slots, far_probs, count)

    size = width // CHUNKS
    spans = [slice(c * size, (c + 1) * size) for c in range(CHUNKS)]

    def send_back(grads, prob, span):
        rows = back(grads, gates, ups, span)
        if span.start == 0:
            column = jnp.broadcast_to(prob.astype(jnp.bfloat16)[:, None], (count, 128))
            rows = jnp.concatenate([rows, column], axis=1)
        return exchange(rows)

    returned = []
    for span in spans:
        rows = send_back(far_grads, far_prob, span)
        partial = combine(far_weighting, rows[:, :size]).astype(jnp.bfloat16)
        returned.append(across(partial))
        if span.start == 0:
            far_values = pick(far_slots, rows[:, size].astype(jnp.float32))
            far_values = across(far_values.astype(jnp.bfloat16))
    pieces = []
    for span, far_piece in zip(spans, returned):
        rows = send_back(near_grads, near_prob, span)
        near_piece = combine(near_weighting, rows[:, :size])
        pieces.append((near_piece + far_piece.astype(jnp.float32)).astype(jnp.bfloat16))
        if span.start == 0:
            near_values = pick(near_slots, rows[:, size].astype(jnp.float32))
    grad_probs = (near_values + far_values.astype(jnp.float32)).astype(jnp.bfloat16)
    return (jnp.concatenate(pieces, axis=1), grad_probs)


def solution(mesh):
    placed = (
        P(("seq", "expert"), None),
        P(("seq", "expert"), None),
        P(("seq", "expert"), None),
        P("expert", None, "seq"),
        P("expert", None, "seq"),
        P("expert", "seq", None),
        P(("seq", "expert"), None),
    )
    return jax.shard_map(
        on_device,
        mesh=mesh,
        in_specs=placed,
        out_specs=(P(("seq", "expert"), None), P(("seq", "expert"), None)),
        check_vma=False,
    )
```

```python
import jax
import jax.numpy as jnp
from jax import lax
from jax.experimental import pallas as pl
from jax.experimental.pallas import tpu as pltpu
from jax.sharding import PartitionSpec as P

CHUNKS = 2
PIECES = 4
STEP = 512
MESH = pl.DeviceIdType.MESH
NT = (((1,), (1,)), ((), ()))


def dot(a, b):
    return jnp.dot(a, b, preferred_element_type=jnp.float32)


def dot_nt(a, b):
    return lax.dot_general(a, b, NT, preferred_element_type=jnp.float32)


def slots_of(routes, base, half, capacity):
    local = routes - base
    chosen = local.reshape(-1)
    onehot = (chosen[:, None] == jnp.arange(half, dtype=jnp.int32)[None, :]).astype(jnp.int32)
    before = jnp.cumsum(onehot, axis=0) - onehot
    position = jnp.sum(before * onehot, axis=1).reshape(routes.shape)
    valid = (local >= 0) & (local < half)
    return jnp.where(valid, local * capacity + position, -1)


def dispatch_of(slots, count):
    lanes = jnp.arange(count, dtype=jnp.int32)[:, None, None]
    return jnp.any(lanes == slots[None], axis=2).astype(jnp.bfloat16)


def weighting_of(slots, probs, count):
    lanes = jnp.arange(count, dtype=jnp.int32)[None, None, :]
    full = jnp.sum(jnp.where(slots[:, :, None] == lanes, probs[:, :, None], 0.0), axis=1)
    high = lax.reduce_precision(full, 8, 7)
    return high.astype(jnp.bfloat16), (full - high).astype(jnp.bfloat16)


def combine(weighting, rows):
    return dot(weighting[0], rows) + dot(weighting[1], rows)


def pick(slots, values):
    lanes = jnp.arange(values.shape[0], dtype=jnp.int32)[None, None, :]
    return jnp.sum(jnp.where(slots[:, :, None] == lanes, values[None, None, :], 0.0), axis=2)


def front(rows_in, gates, ups):
    return [(dot(rows_in, g), dot(rows_in, u)) for g, u in zip(gates, ups)]


def middle(terms, rows_grad, downs):
    prob, grads = 0.0, []
    for (gating, lifted), d in zip(terms, downs):
        sigmoid = jax.nn.sigmoid(gating)
        active = gating * sigmoid
        hidden = (active * lifted).astype(jnp.bfloat16)
        grad_hidden = dot_nt(rows_grad, d)
        prob = prob + jnp.sum(hidden.astype(jnp.float32) * grad_hidden, axis=1)
        slope_term = sigmoid * (1.0 + gating * (1.0 - sigmoid))
        grads.append(
            (
                (grad_hidden * lifted * slope_term).astype(jnp.bfloat16),
                (grad_hidden * active).astype(jnp.bfloat16),
            )
        )
    return grads, prob


def back(grads, gates, ups, columns):
    total = 0.0
    for (gg, gu), g, u in zip(grads, gates, ups):
        total = total + dot_nt(gg, g[columns]) + dot_nt(gu, u[columns])
    return total.astype(jnp.bfloat16)


def halves_on_device(tokens, routes, route_probs, gate_weight, up_weight, down_weight, grad_out):
    tok_count, width = tokens.shape
    top_count = routes.shape[1]
    experts = lax.axis_size("expert")
    parts = lax.axis_size("seq")
    capacity = 3 * tok_count * top_count // (2 * experts)
    half = experts // 2
    count = half * capacity
    base = (lax.axis_index("expert") // half) * half
    swap = [(i, (i + half) % experts) for i in range(experts)]
    groups = [list(range(half)), list(range(half, experts))]

    def across(value):
        return lax.ppermute(value, "expert", swap)

    def exchange(value):
        value = value.reshape(half, capacity, -1)
        value = lax.all_to_all(
            value, "expert", split_axis=0, concat_axis=0, tiled=True, axis_index_groups=groups
        )
        return value.reshape(count, -1)

    far_routes, far_probs = across(routes), across(route_probs)
    far_tokens, far_grad = across(tokens), across(grad_out)

    gates, ups, downs = [gate_weight[0]], [up_weight[0]], [down_weight[0]]
    for shift in range(1, parts):
        turn = [(i, (i + shift) % parts) for i in range(parts)]
        gates.append(lax.ppermute(gate_weight[0], "seq", turn))
        ups.append(lax.ppermute(up_weight[0], "seq", turn))
        downs.append(lax.ppermute(down_weight[0], "seq", turn))

    near_slots = slots_of(routes, base, half, capacity)
    near_pick = dispatch_of(near_slots, count)
    near_in = exchange(dot(near_pick, tokens).astype(jnp.bfloat16))
    near_out = exchange(dot(near_pick, grad_out).astype(jnp.bfloat16))
    near_grads, near_prob = middle(front(near_in, gates, ups), near_out, downs)

    far_slots = slots_of(far_routes, base, half, capacity)
    far_pick = dispatch_of(far_slots, count)
    far_in = exchange(dot(far_pick, far_tokens).astype(jnp.bfloat16))
    far_terms = front(far_in, gates, ups)
    far_out = exchange(dot(far_pick, far_grad).astype(jnp.bfloat16))
    far_grads, far_prob = middle(far_terms, far_out, downs)

    near_weighting = weighting_of(near_slots, route_probs, count)
    far_weighting = weighting_of(far_slots, far_probs, count)

    size = width // CHUNKS
    spans = [slice(c * size, (c + 1) * size) for c in range(CHUNKS)]

    def send_back(grads, prob, span):
        rows = back(grads, gates, ups, span)
        if span.start == 0:
            column = jnp.broadcast_to(prob.astype(jnp.bfloat16)[:, None], (count, 128))
            rows = jnp.concatenate([rows, column], axis=1)
        return exchange(rows)

    returned = []
    for span in spans:
        rows = send_back(far_grads, far_prob, span)
        partial = combine(far_weighting, rows[:, :size]).astype(jnp.bfloat16)
        returned.append(across(partial))
        if span.start == 0:
            far_values = pick(far_slots, rows[:, size].astype(jnp.float32))
            far_values = across(far_values.astype(jnp.bfloat16))
    pieces = []
    for span, far_piece in zip(spans, returned):
        rows = send_back(near_grads, near_prob, span)
        near_piece = combine(near_weighting, rows[:, :size])
        pieces.append((near_piece + far_piece.astype(jnp.float32)).astype(jnp.bfloat16))
        if span.start == 0:
            near_values = pick(near_slots, rows[:, size].astype(jnp.float32))
    grad_probs = (near_values + far_values.astype(jnp.float32)).astype(jnp.bfloat16)
    return (jnp.concatenate(pieces, axis=1), grad_probs)


def fused_kernel(
    half,
    tokens, grads, near_pick, far_pick_out, near_mats, far_mats_out, gate_hbm, up_hbm, down_hbm,
    out, probs_out,
    far_pick, far_mats, far_tok, gate_w, up_w, down_w, send, recv, acc, grad_hid,
    back_send, back_recv, prob_send, prob_recv, part_send, part_recv, val_send, val_recv,
    local_sem, x_send, x_recv, w_send, w_recv, a_send, a_recv, b_send, b_recv, p_send, p_recv,
    y_send, y_recv, v_send, v_recv,
):
    tok_count, width = tokens.shape
    capacity = send.shape[2]
    count = half * capacity
    hid = acc.shape[3]
    piece = width // PIECES
    me = lax.axis_index("expert")
    core = lax.axis_index("seq")
    base = (me // half) * half
    mine = me - base
    partner = {"expert": lax.rem(me + half, 2 * half)}
    twin = {"seq": 1 - core}
    peers = [lax.rem(mine + d, half) for d in range(half)]

    def remote(src, dst, ss, rs, device):
        return pltpu.make_async_remote_copy(
            src_ref=src, dst_ref=dst, send_sem=ss, recv_sem=rs,
            device_id=device, device_id_type=MESH,
        )

    locals_ = [
        pltpu.make_async_copy(src.at[0], dst.at[0], local_sem.at[i])
        for i, (src, dst) in enumerate(((gate_hbm, gate_w), (up_hbm, up_w), (down_hbm, down_w)))
    ]
    for copy in locals_:
        copy.start()

    barrier = pltpu.get_barrier_semaphore()
    pl.semaphore_signal(barrier, inc=1, device_id=partner, device_id_type=MESH)
    pl.semaphore_signal(barrier, inc=1, device_id=twin, device_id_type=MESH)
    for d in range(1, half):
        pl.semaphore_signal(
            barrier, inc=1, device_id={"expert": base + peers[d]}, device_id_type=MESH
        )
    pl.semaphore_wait(barrier, half + 1)

    crossing = [
        remote(far_pick_out, far_pick, x_send.at[0], x_recv.at[0], partner),
        remote(tokens, far_tok.at[0], x_send.at[1], x_recv.at[1], partner),
        remote(grads, far_tok.at[1], x_send.at[2], x_recv.at[2], partner),
        remote(far_mats_out, far_mats, x_send.at[3], x_recv.at[3], partner),
    ]
    for copy in crossing:
        copy.start()
    swaps = [
        remote(src.at[0], dst.at[1], w_send.at[i], w_recv.at[i], twin)
        for i, (src, dst) in enumerate(((gate_hbm, gate_w), (up_hbm, up_w), (down_hbm, down_w)))
    ]
    for copy in swaps:
        copy.start()

    def dispatch(pick, source, stream):
        @pl.loop(0, width // STEP)
        def _(k):
            cols = pl.ds(pl.multiple_of(k * STEP, STEP), STEP)
            rows = dot(pick[...], source[:, cols])
            send[stream, :, :, cols] = rows.reshape(half, capacity, STEP).astype(jnp.bfloat16)

        copies = [
            remote(
                send.at[stream, peers[d]], recv.at[stream, mine],
                a_send.at[stream, d], a_recv.at[stream, d], {"expert": base + peers[d]},
            )
            for d in range(1, half)
        ]
        for copy in copies:
            copy.start()
        recv[stream, mine] = send[stream, mine]
        return copies

    def rows_of(buffer, cols):
        block = buffer[:, :, cols].astype(jnp.float32)
        return block.reshape(count, block.shape[2]).astype(jnp.bfloat16)

    def front_in(stream):
        acc[0] = jnp.zeros(acc.shape[1:], jnp.float32)
        acc[1] = jnp.zeros(acc.shape[1:], jnp.float32)

        @pl.loop(0, width // STEP)
        def _(k):
            cols = pl.ds(pl.multiple_of(k * STEP, STEP), STEP)
            rows = rows_of(recv.at[stream], cols)
            for j in range(2):
                acc[0, j] += dot(rows, gate_w[j, cols, :])
                acc[1, j] += dot(rows, up_w[j, cols, :])

    def front_out(stream):
        acc[2] = jnp.zeros(acc.shape[1:], jnp.float32)

        @pl.loop(0, width // STEP)
        def _(k):
            cols = pl.ds(pl.multiple_of(k * STEP, STEP), STEP)
            rows = rows_of(recv.at[stream], cols)
            for j in range(2):
                acc[2, j] += dot_nt(rows, down_w[j, :, cols])

    def pointwise(which):
        prob = jnp.zeros((count, 1), jnp.float32)
        for j in range(2):
            gating, lifted, grad_hidden = acc[0, j], acc[1, j], acc[2, j]
            sigmoid = jax.nn.sigmoid(gating)
            active = gating * sigmoid
            hidden = (active * lifted).astype(jnp.bfloat16)
            prob += jnp.sum(hidden.astype(jnp.float32) * grad_hidden, axis=1, keepdims=True)
            slope_term = sigmoid * (1.0 + gating * (1.0 - sigmoid))
            grad_hid[which, 0, j] = (grad_hidden * lifted * slope_term).astype(jnp.bfloat16)
            grad_hid[which, 1, j] = (grad_hidden * active).astype(jnp.bfloat16)
        wide = jnp.broadcast_to(prob, (count, 128)).reshape(half, capacity, 128)
        prob_send[which] = wide.astype(jnp.bfloat16)

    def return_probs(which):
        copies = [
            remote(
                prob_send.at[which, peers[d]], prob_recv.at[which, mine],
                p_send.at[which, d], p_recv.at[which, d], {"expert": base + peers[d]},
            )
            for d in range(1, half)
        ]
        for copy in copies:
            copy.start()
        prob_recv[which, mine] = prob_send[which, mine]
        return copies

    def return_rows(which, c):
        @pl.loop(0, piece // STEP)
        def _(k):
            cols = pl.ds(pl.multiple_of(c * piece + k * STEP, STEP), STEP)
            total = dot_nt(grad_hid[which, 0, 0], gate_w[0, cols, :])
            total += dot_nt(grad_hid[which, 0, 1], gate_w[1, cols, :])
            total += dot_nt(grad_hid[which, 1, 0], up_w[0, cols, :])
            total += dot_nt(grad_hid[which, 1, 1], up_w[1, cols, :])
            inner = pl.ds(pl.multiple_of(k * STEP, STEP), STEP)
            back_send[which, c, :, :, inner] = total.reshape(half, capacity, STEP).astype(
                jnp.bfloat16
            )

        copies = [
            remote(
                back_send.at[which, c, peers[d]], back_recv.at[which, c, mine],
                b_send.at[which, c, d], b_recv.at[which, c, d], {"expert": base + peers[d]},
            )
            for d in range(1, half)
        ]
        for copy in copies:
            copy.start()
        back_recv[which, c, mine] = back_send[which, c, mine]
        return copies

    def arrived(copies):
        for copy in copies:
            copy.wait_recv()

    whole = pl.ds(0, 128)
    near = [dispatch(near_pick, tokens, 0), dispatch(near_pick, grads, 1)]
    for copy in locals_:
        copy.wait()
    arrived(swaps)
    arrived(near[0])
    front_in(0)
    crossing[0].wait_recv()
    crossing[1].wait_recv()
    far = [dispatch(far_pick, far_tok.at[0], 2)]
    arrived(near[1])
    front_out(1)
    pointwise(0)
    arrived(far[0])
    front_in(2)
    crossing[2].wait_recv()
    far.append(dispatch(far_pick, far_tok.at[1], 3))
    near_probs = return_probs(0)
    crossing[3].wait_recv()
    arrived(far[1])
    front_out(3)
    pointwise(1)

    far_back, partials = [], []

    def forward_piece(c):
        arrived(far_back[c])

        @pl.loop(0, piece // STEP)
        def _(k):
            inner = pl.ds(pl.multiple_of(k * STEP, STEP), STEP)
            rows = rows_of(back_recv.at[1, c], inner)
            part_send[c, :, inner] = (dot(far_mats[2], rows) + dot(far_mats[3], rows)).astype(
                jnp.bfloat16
            )

        copy = remote(part_send.at[c], part_recv.at[c], y_send.at[c], y_recv.at[c], partner)
        copy.start()
        partials.append(copy)

    for c in range(PIECES):
        far_back.append(return_rows(1, c))
        if c:
            forward_piece(c - 1)
    far_probs = return_probs(1)
    forward_piece(PIECES - 1)
    arrived(far_probs)
    far_rows = rows_of(prob_recv.at[1], whole)
    val_send[0] = dot(far_mats[0], far_rows).astype(jnp.bfloat16)
    val_send[1] = dot(far_mats[1], far_rows).astype(jnp.bfloat16)
    values = remote(val_send, val_recv, v_send.at[0], v_recv.at[0], partner)
    values.start()

    near_back = [return_rows(0, c) for c in range(PIECES)]
    for c in range(PIECES):
        arrived(near_back[c])
        arrived([partials[c]])

        @pl.loop(0, piece // STEP)
        def _(k):
            inner = pl.ds(pl.multiple_of(k * STEP, STEP), STEP)
            rows = rows_of(back_recv.at[0, c], inner)
            total = dot(near_mats[2], rows) + dot(near_mats[3], rows)
            total += part_recv[c, :, inner].astype(jnp.float32)
            cols = pl.ds(pl.multiple_of(c * piece + k * STEP, STEP), STEP)
            out[:, cols] = total.astype(jnp.bfloat16)

    arrived(near_probs)
    arrived([values])
    near_rows = rows_of(prob_recv.at[0], whole)
    for k in range(2):
        total = dot(near_mats[k], near_rows) + val_recv[k].astype(jnp.float32)
        probs_out[k] = total.astype(jnp.bfloat16)
    groups = [crossing, swaps, *near, *far, near_probs, far_probs, partials, [values]]
    for copies in groups + far_back + near_back:
        for copy in copies:
            copy.wait_send()


def fused_on_device(tokens, routes, route_probs, gate_weight, up_weight, down_weight, grad_out):
    tok_count, width = tokens.shape
    top_count = routes.shape[1]
    experts = lax.axis_size("expert")
    capacity = 3 * tok_count * top_count // (2 * experts)
    half = experts // 2
    count = half * capacity
    hid = gate_weight.shape[2]
    base = (lax.axis_index("expert") // half) * half

    def tables(first):
        slots = slots_of(routes, first, half, capacity)
        lanes = jnp.arange(count, dtype=jnp.int32)[None, None, :]
        chosen = (slots.T[:, :, None] == lanes).astype(jnp.bfloat16)
        high, low = weighting_of(slots, route_probs, count)
        return dispatch_of(slots, count), jnp.concatenate([chosen, jnp.stack([high, low])], axis=0)

    near_pick, near_mats = tables(base)
    far_pick, far_mats = tables(experts - half - base)
    vmem, sems = pltpu.VMEM, pltpu.SemaphoreType.DMA
    bf16 = jnp.bfloat16
    piece = width // PIECES
    spec = pl.BlockSpec(memory_space=pltpu.VMEM)
    raw = pl.BlockSpec(memory_space=pl.ANY)
    grad_tokens, values = pl.pallas_call(
        lambda *refs: fused_kernel(half, *refs),
        name="routed_backward",
        out_shape=(
            jax.ShapeDtypeStruct((tok_count, width), bf16),
            jax.ShapeDtypeStruct((2, tok_count, 128), bf16),
        ),
        in_specs=[spec] * 6 + [raw] * 3,
        out_specs=(spec, spec),
        scratch_shapes=[
            vmem((count, tok_count), bf16),
            vmem((4, tok_count, count), bf16),
            vmem((2, tok_count, width), bf16),
            vmem((2, width, hid), bf16),
            vmem((2, width, hid), bf16),
            vmem((2, hid, width), bf16),
            vmem((4, half, capacity, width), bf16),
            vmem((4, half, capacity, width), bf16),
            vmem((3, 2, count, hid), jnp.float32),
            vmem((2, 2, 2, count, hid), bf16),
            vmem((2, PIECES, half, capacity, piece), bf16),
            vmem((2, PIECES, half, capacity, piece), bf16),
            vmem((2, half, capacity, 128), bf16),
            vmem((2, half, capacity, 128), bf16),
            vmem((PIECES, tok_count, piece), bf16),
            vmem((PIECES, tok_count, piece), bf16),
            vmem((2, tok_count, 128), bf16),
            vmem((2, tok_count, 128), bf16),
            sems((3,)),
            sems((4,)), sems((4,)),
            sems((3,)), sems((3,)),
            sems((4, half)), sems((4, half)),
            sems((2, PIECES, half)), sems((2, PIECES, half)),
            sems((2, half)), sems((2, half)),
            sems((PIECES,)), sems((PIECES,)),
            sems((1,)), sems((1,)),
        ],
        compiler_params=pltpu.CompilerParams(
            collective_id=0, has_side_effects=True, vmem_limit_bytes=63 * 1024 * 1024
        ),
    )(
        tokens, grad_out, near_pick, far_pick, near_mats, far_mats,
        gate_weight, up_weight, down_weight,
    )
    return grad_tokens, values[:, :, 0].T


def on_device(tokens, routes, *rest):
    experts = lax.axis_size("expert")
    capacity = 3 * routes.shape[0] * routes.shape[1] // (2 * experts)
    fits = capacity % 8 == 0 and lax.axis_size("seq") == 2 and routes.shape[1] == 2
    run = fused_on_device if fits else halves_on_device
    return run(tokens, routes, *rest)


def solution(mesh):
    placed = (
        P(("seq", "expert"), None),
        P(("seq", "expert"), None),
        P(("seq", "expert"), None),
        P("expert", None, "seq"),
        P("expert", None, "seq"),
        P("expert", "seq", None),
        P(("seq", "expert"), None),
    )
    return jax.shard_map(
        on_device,
        mesh=mesh,
        in_specs=placed,
        out_specs=(P(("seq", "expert"), None), P(("seq", "expert"), None)),
        check_vma=False,
    )
```

```python
import jax
import jax.numpy as jnp
from jax import lax
from jax.experimental import pallas as pl
from jax.experimental.pallas import tpu as pltpu
from jax.sharding import PartitionSpec as P

CHUNKS = 2
PIECES = 4
STEP = 512
MESH = pl.DeviceIdType.MESH
NT = (((1,), (1,)), ((), ()))


def dot(a, b):
    return jnp.dot(a, b, preferred_element_type=jnp.float32)


def dot_nt(a, b):
    return lax.dot_general(a, b, NT, preferred_element_type=jnp.float32)


def slots_of(routes, base, half, capacity):
    local = routes - base
    chosen = local.reshape(-1)
    onehot = (chosen[:, None] == jnp.arange(half, dtype=jnp.int32)[None, :]).astype(jnp.int32)
    before = jnp.cumsum(onehot, axis=0) - onehot
    position = jnp.sum(before * onehot, axis=1).reshape(routes.shape)
    valid = (local >= 0) & (local < half)
    return jnp.where(valid, local * capacity + position, -1)


def dispatch_of(slots, count):
    lanes = jnp.arange(count, dtype=jnp.int32)[:, None, None]
    return jnp.any(lanes == slots[None], axis=2).astype(jnp.bfloat16)


def weighting_of(slots, probs, count):
    lanes = jnp.arange(count, dtype=jnp.int32)[None, None, :]
    full = jnp.sum(jnp.where(slots[:, :, None] == lanes, probs[:, :, None], 0.0), axis=1)
    high = lax.reduce_precision(full, 8, 7)
    return high.astype(jnp.bfloat16), (full - high).astype(jnp.bfloat16)


def combine(weighting, rows):
    return dot(weighting[0], rows) + dot(weighting[1], rows)


def pick(slots, values):
    lanes = jnp.arange(values.shape[0], dtype=jnp.int32)[None, None, :]
    return jnp.sum(jnp.where(slots[:, :, None] == lanes, values[None, None, :], 0.0), axis=2)


def front(rows_in, gates, ups):
    return [(dot(rows_in, g), dot(rows_in, u)) for g, u in zip(gates, ups)]


def middle(terms, rows_grad, downs):
    prob, grads = 0.0, []
    for (gating, lifted), d in zip(terms, downs):
        sigmoid = jax.nn.sigmoid(gating)
        active = gating * sigmoid
        hidden = (active * lifted).astype(jnp.bfloat16)
        grad_hidden = dot_nt(rows_grad, d)
        prob = prob + jnp.sum(hidden.astype(jnp.float32) * grad_hidden, axis=1)
        slope_term = sigmoid * (1.0 + gating * (1.0 - sigmoid))
        grads.append(
            (
                (grad_hidden * lifted * slope_term).astype(jnp.bfloat16),
                (grad_hidden * active).astype(jnp.bfloat16),
            )
        )
    return grads, prob


def back(grads, gates, ups, columns):
    total = 0.0
    for (gg, gu), g, u in zip(grads, gates, ups):
        total = total + dot_nt(gg, g[columns]) + dot_nt(gu, u[columns])
    return total.astype(jnp.bfloat16)


def halves_on_device(tokens, routes, route_probs, gate_weight, up_weight, down_weight, grad_out):
    tok_count, width = tokens.shape
    top_count = routes.shape[1]
    experts = lax.axis_size("expert")
    parts = lax.axis_size("seq")
    capacity = 3 * tok_count * top_count // (2 * experts)
    half = experts // 2
    count = half * capacity
    base = (lax.axis_index("expert") // half) * half
    swap = [(i, (i + half) % experts) for i in range(experts)]
    groups = [list(range(half)), list(range(half, experts))]

    def across(value):
        return lax.ppermute(value, "expert", swap)

    def exchange(value):
        value = value.reshape(half, capacity, -1)
        value = lax.all_to_all(
            value, "expert", split_axis=0, concat_axis=0, tiled=True, axis_index_groups=groups
        )
        return value.reshape(count, -1)

    far_routes, far_probs = across(routes), across(route_probs)
    far_tokens, far_grad = across(tokens), across(grad_out)

    gates, ups, downs = [gate_weight[0]], [up_weight[0]], [down_weight[0]]
    for shift in range(1, parts):
        turn = [(i, (i + shift) % parts) for i in range(parts)]
        gates.append(lax.ppermute(gate_weight[0], "seq", turn))
        ups.append(lax.ppermute(up_weight[0], "seq", turn))
        downs.append(lax.ppermute(down_weight[0], "seq", turn))

    near_slots = slots_of(routes, base, half, capacity)
    near_pick = dispatch_of(near_slots, count)
    near_in = exchange(dot(near_pick, tokens).astype(jnp.bfloat16))
    near_out = exchange(dot(near_pick, grad_out).astype(jnp.bfloat16))
    near_grads, near_prob = middle(front(near_in, gates, ups), near_out, downs)

    far_slots = slots_of(far_routes, base, half, capacity)
    far_pick = dispatch_of(far_slots, count)
    far_in = exchange(dot(far_pick, far_tokens).astype(jnp.bfloat16))
    far_terms = front(far_in, gates, ups)
    far_out = exchange(dot(far_pick, far_grad).astype(jnp.bfloat16))
    far_grads, far_prob = middle(far_terms, far_out, downs)

    near_weighting = weighting_of(near_slots, route_probs, count)
    far_weighting = weighting_of(far_slots, far_probs, count)

    size = width // CHUNKS
    spans = [slice(c * size, (c + 1) * size) for c in range(CHUNKS)]

    def send_back(grads, prob, span):
        rows = back(grads, gates, ups, span)
        if span.start == 0:
            column = jnp.broadcast_to(prob.astype(jnp.bfloat16)[:, None], (count, 128))
            rows = jnp.concatenate([rows, column], axis=1)
        return exchange(rows)

    returned = []
    for span in spans:
        rows = send_back(far_grads, far_prob, span)
        partial = combine(far_weighting, rows[:, :size]).astype(jnp.bfloat16)
        returned.append(across(partial))
        if span.start == 0:
            far_values = pick(far_slots, rows[:, size].astype(jnp.float32))
            far_values = across(far_values.astype(jnp.bfloat16))
    pieces = []
    for span, far_piece in zip(spans, returned):
        rows = send_back(near_grads, near_prob, span)
        near_piece = combine(near_weighting, rows[:, :size])
        pieces.append((near_piece + far_piece.astype(jnp.float32)).astype(jnp.bfloat16))
        if span.start == 0:
            near_values = pick(near_slots, rows[:, size].astype(jnp.float32))
    grad_probs = (near_values + far_values.astype(jnp.float32)).astype(jnp.bfloat16)
    return (jnp.concatenate(pieces, axis=1), grad_probs)


def fused_kernel(
    half,
    tokens, grads, near_pick, far_pick_out, near_mats, far_mats_out, gate_hbm, up_hbm, down_hbm,
    out, probs_out,
    far_pick, far_mats, far_tok, gate_w, up_w, down_w, send, recv, acc, grad_hid,
    back_send, back_recv, prob_send, prob_recv, part_send, part_recv, val_send, val_recv,
    local_sem, x_send, x_recv, w_send, w_recv, a_send, a_recv, b_send, b_recv, p_send, p_recv,
    y_send, y_recv, v_send, v_recv,
):
    tok_count, width = tokens.shape
    capacity = send.shape[2]
    count = half * capacity
    hid = acc.shape[3]
    piece, middle = width // PIECES, width // 2
    me = lax.axis_index("expert")
    core = lax.axis_index("seq")
    base = (me // half) * half
    mine = me - base
    partner = {"expert": lax.rem(me + half, 2 * half)}
    twin = {"seq": 1 - core}
    peers = [lax.rem(mine + d, half) for d in range(half)]

    def remote(src, dst, ss, rs, device):
        return pltpu.make_async_remote_copy(
            src_ref=src, dst_ref=dst, send_sem=ss, recv_sem=rs,
            device_id=device, device_id_type=MESH,
        )

    locals_ = [
        pltpu.make_async_copy(src.at[0], dst.at[0], local_sem.at[i])
        for i, (src, dst) in enumerate(((gate_hbm, gate_w), (up_hbm, up_w), (down_hbm, down_w)))
    ]
    for copy in locals_:
        copy.start()

    barrier = pltpu.get_barrier_semaphore()
    pl.semaphore_signal(barrier, inc=1, device_id=partner, device_id_type=MESH)
    pl.semaphore_signal(barrier, inc=1, device_id=twin, device_id_type=MESH)
    for d in range(1, half):
        pl.semaphore_signal(
            barrier, inc=1, device_id={"expert": base + peers[d]}, device_id_type=MESH
        )
    pl.semaphore_wait(barrier, half + 1)

    crossing = [
        remote(far_pick_out, far_pick, x_send.at[0], x_recv.at[0], partner),
        remote(tokens, far_tok.at[0], x_send.at[1], x_recv.at[1], partner),
        remote(
            grads.at[:, :middle], far_tok.at[1, :, :middle], x_send.at[2], x_recv.at[2], partner
        ),
        remote(
            grads.at[:, middle:], far_tok.at[1, :, middle:], x_send.at[3], x_recv.at[3], partner
        ),
        remote(far_mats_out, far_mats, x_send.at[4], x_recv.at[4], partner),
    ]
    for copy in crossing[:2]:
        copy.start()
    swaps = [
        remote(src.at[0], dst.at[1], w_send.at[i], w_recv.at[i], twin)
        for i, (src, dst) in enumerate(((gate_hbm, gate_w), (up_hbm, up_w), (down_hbm, down_w)))
    ]
    for copy in swaps:
        copy.start()

    def dispatch(pick, source, stream, lane, start, size):
        @pl.loop(start // STEP, (start + size) // STEP)
        def _(k):
            cols = pl.ds(pl.multiple_of(k * STEP, STEP), STEP)
            rows = dot(pick[...], source[:, cols])
            send[stream, :, :, cols] = rows.reshape(half, capacity, STEP).astype(jnp.bfloat16)

        copies = [
            remote(
                send.at[stream, peers[d], :, start : start + size],
                recv.at[stream, mine, :, start : start + size],
                a_send.at[lane, d], a_recv.at[lane, d], {"expert": base + peers[d]},
            )
            for d in range(1, half)
        ]
        for copy in copies:
            copy.start()
        own = pl.ds(start, size)
        recv[stream, mine, :, own] = send[stream, mine, :, own]
        return copies

    def rows_of(buffer, cols):
        block = buffer[:, :, cols].astype(jnp.float32)
        return block.reshape(count, block.shape[2]).astype(jnp.bfloat16)

    def front_in(stream):
        acc[0] = jnp.zeros(acc.shape[1:], jnp.float32)
        acc[1] = jnp.zeros(acc.shape[1:], jnp.float32)

        @pl.loop(0, width // STEP)
        def _(k):
            cols = pl.ds(pl.multiple_of(k * STEP, STEP), STEP)
            rows = rows_of(recv.at[stream], cols)
            for j in range(2):
                acc[0, j] += dot(rows, gate_w[j, cols, :])
                acc[1, j] += dot(rows, up_w[j, cols, :])

    def front_out(stream, start, size):
        if start == 0:
            acc[2] = jnp.zeros(acc.shape[1:], jnp.float32)

        @pl.loop(start // STEP, (start + size) // STEP)
        def _(k):
            cols = pl.ds(pl.multiple_of(k * STEP, STEP), STEP)
            rows = rows_of(recv.at[stream], cols)
            for j in range(2):
                acc[2, j] += dot_nt(rows, down_w[j, :, cols])

    def pointwise(which):
        prob = jnp.zeros((count, 1), jnp.float32)
        for j in range(2):
            gating, lifted, grad_hidden = acc[0, j], acc[1, j], acc[2, j]
            sigmoid = jax.nn.sigmoid(gating)
            active = gating * sigmoid
            hidden = (active * lifted).astype(jnp.bfloat16)
            prob += jnp.sum(hidden.astype(jnp.float32) * grad_hidden, axis=1, keepdims=True)
            slope_term = sigmoid * (1.0 + gating * (1.0 - sigmoid))
            grad_hid[which, 0, j] = (grad_hidden * lifted * slope_term).astype(jnp.bfloat16)
            grad_hid[which, 1, j] = (grad_hidden * active).astype(jnp.bfloat16)
        wide = jnp.broadcast_to(prob, (count, 128)).reshape(half, capacity, 128)
        prob_send[which] = wide.astype(jnp.bfloat16)

    def return_probs(which):
        copies = [
            remote(
                prob_send.at[which, peers[d]], prob_recv.at[which, mine],
                p_send.at[which, d], p_recv.at[which, d], {"expert": base + peers[d]},
            )
            for d in range(1, half)
        ]
        for copy in copies:
            copy.start()
        prob_recv[which, mine] = prob_send[which, mine]
        return copies

    def return_rows(which, c):
        @pl.loop(0, piece // STEP)
        def _(k):
            cols = pl.ds(pl.multiple_of(c * piece + k * STEP, STEP), STEP)
            total = dot_nt(grad_hid[which, 0, 0], gate_w[0, cols, :])
            total += dot_nt(grad_hid[which, 0, 1], gate_w[1, cols, :])
            total += dot_nt(grad_hid[which, 1, 0], up_w[0, cols, :])
            total += dot_nt(grad_hid[which, 1, 1], up_w[1, cols, :])
            inner = pl.ds(pl.multiple_of(k * STEP, STEP), STEP)
            back_send[which, c, :, :, inner] = total.reshape(half, capacity, STEP).astype(
                jnp.bfloat16
            )

        copies = [
            remote(
                back_send.at[which, c, peers[d]], back_recv.at[which, c, mine],
                b_send.at[which, c, d], b_recv.at[which, c, d], {"expert": base + peers[d]},
            )
            for d in range(1, half)
        ]
        for copy in copies:
            copy.start()
        back_recv[which, c, mine] = back_send[which, c, mine]
        return copies

    def arrived(copies):
        for copy in copies:
            copy.wait_recv()

    whole = pl.ds(0, 128)
    near = [
        dispatch(near_pick, tokens, 0, 0, 0, width),
        dispatch(near_pick, grads, 1, 1, 0, width),
    ]
    for copy in crossing[2:]:
        copy.start()
    crossing[0].wait_recv()
    crossing[1].wait_recv()
    far = [dispatch(far_pick, far_tok.at[0], 2, 2, 0, width)]
    for copy in locals_:
        copy.wait()
    arrived(swaps)
    arrived(near[0])
    front_in(0)
    arrived(near[1])
    front_out(1, 0, width)
    pointwise(0)
    near_probs = return_probs(0)
    near_back = [return_rows(0, c) for c in range(PIECES // 2)]
    crossing[2].wait_recv()
    far.append(dispatch(far_pick, far_tok.at[1], 3, 3, 0, middle))
    arrived(far[0])
    front_in(2)
    crossing[3].wait_recv()
    far.append(dispatch(far_pick, far_tok.at[1], 3, 4, middle, middle))
    crossing[4].wait_recv()
    arrived(far[1])
    front_out(3, 0, middle)
    arrived(far[2])
    front_out(3, middle, middle)
    pointwise(1)

    far_back, partials = [], []

    def forward_piece(c):
        arrived(far_back[c])

        @pl.loop(0, piece // STEP)
        def _(k):
            inner = pl.ds(pl.multiple_of(k * STEP, STEP), STEP)
            rows = rows_of(back_recv.at[1, c], inner)
            part_send[c, :, inner] = (dot(far_mats[2], rows) + dot(far_mats[3], rows)).astype(
                jnp.bfloat16
            )

        copy = remote(part_send.at[c], part_recv.at[c], y_send.at[c], y_recv.at[c], partner)
        copy.start()
        partials.append(copy)

    for c in range(PIECES):
        far_back.append(return_rows(1, c))
        if c:
            forward_piece(c - 1)
    far_probs = return_probs(1)
    forward_piece(PIECES - 1)
    arrived(far_probs)
    far_rows = rows_of(prob_recv.at[1], whole)
    val_send[0] = dot(far_mats[0], far_rows).astype(jnp.bfloat16)
    val_send[1] = dot(far_mats[1], far_rows).astype(jnp.bfloat16)
    values = remote(val_send, val_recv, v_send.at[0], v_recv.at[0], partner)
    values.start()

    near_back += [return_rows(0, c) for c in range(PIECES // 2, PIECES)]
    for c in range(PIECES):
        arrived(near_back[c])
        arrived([partials[c]])

        @pl.loop(0, piece // STEP)
        def _(k):
            inner = pl.ds(pl.multiple_of(k * STEP, STEP), STEP)
            rows = rows_of(back_recv.at[0, c], inner)
            total = dot(near_mats[2], rows) + dot(near_mats[3], rows)
            total += part_recv[c, :, inner].astype(jnp.float32)
            cols = pl.ds(pl.multiple_of(c * piece + k * STEP, STEP), STEP)
            out[:, cols] = total.astype(jnp.bfloat16)

    arrived(near_probs)
    arrived([values])
    near_rows = rows_of(prob_recv.at[0], whole)
    for k in range(2):
        total = dot(near_mats[k], near_rows) + val_recv[k].astype(jnp.float32)
        probs_out[k] = total.astype(jnp.bfloat16)
    groups = [crossing, swaps, *near, *far, near_probs, far_probs, partials, [values]]
    for copies in groups + far_back + near_back:
        for copy in copies:
            copy.wait_send()


def fused_on_device(tokens, routes, route_probs, gate_weight, up_weight, down_weight, grad_out):
    tok_count, width = tokens.shape
    top_count = routes.shape[1]
    experts = lax.axis_size("expert")
    capacity = 3 * tok_count * top_count // (2 * experts)
    half = experts // 2
    count = half * capacity
    hid = gate_weight.shape[2]
    base = (lax.axis_index("expert") // half) * half

    def tables(first):
        slots = slots_of(routes, first, half, capacity)
        lanes = jnp.arange(count, dtype=jnp.int32)[None, None, :]
        chosen = (slots.T[:, :, None] == lanes).astype(jnp.bfloat16)
        high, low = weighting_of(slots, route_probs, count)
        return dispatch_of(slots, count), jnp.concatenate([chosen, jnp.stack([high, low])], axis=0)

    near_pick, near_mats = tables(base)
    far_pick, far_mats = tables(experts - half - base)
    vmem, sems = pltpu.VMEM, pltpu.SemaphoreType.DMA
    bf16 = jnp.bfloat16
    piece = width // PIECES
    spec = pl.BlockSpec(memory_space=pltpu.VMEM)
    raw = pl.BlockSpec(memory_space=pl.ANY)
    grad_tokens, values = pl.pallas_call(
        lambda *refs: fused_kernel(half, *refs),
        name="routed_backward",
        out_shape=(
            jax.ShapeDtypeStruct((tok_count, width), bf16),
            jax.ShapeDtypeStruct((2, tok_count, 128), bf16),
        ),
        in_specs=[spec] * 6 + [raw] * 3,
        out_specs=(spec, spec),
        scratch_shapes=[
            vmem((count, tok_count), bf16),
            vmem((4, tok_count, count), bf16),
            vmem((2, tok_count, width), bf16),
            vmem((2, width, hid), bf16),
            vmem((2, width, hid), bf16),
            vmem((2, hid, width), bf16),
            vmem((4, half, capacity, width), bf16),
            vmem((4, half, capacity, width), bf16),
            vmem((3, 2, count, hid), jnp.float32),
            vmem((2, 2, 2, count, hid), bf16),
            vmem((2, PIECES, half, capacity, piece), bf16),
            vmem((2, PIECES, half, capacity, piece), bf16),
            vmem((2, half, capacity, 128), bf16),
            vmem((2, half, capacity, 128), bf16),
            vmem((PIECES, tok_count, piece), bf16),
            vmem((PIECES, tok_count, piece), bf16),
            vmem((2, tok_count, 128), bf16),
            vmem((2, tok_count, 128), bf16),
            sems((3,)),
            sems((5,)), sems((5,)),
            sems((3,)), sems((3,)),
            sems((5, half)), sems((5, half)),
            sems((2, PIECES, half)), sems((2, PIECES, half)),
            sems((2, half)), sems((2, half)),
            sems((PIECES,)), sems((PIECES,)),
            sems((1,)), sems((1,)),
        ],
        compiler_params=pltpu.CompilerParams(
            collective_id=0, has_side_effects=True, vmem_limit_bytes=63 * 1024 * 1024
        ),
    )(
        tokens, grad_out, near_pick, far_pick, near_mats, far_mats,
        gate_weight, up_weight, down_weight,
    )
    return grad_tokens, values[:, :, 0].T


def on_device(tokens, routes, *rest):
    experts = lax.axis_size("expert")
    capacity = 3 * routes.shape[0] * routes.shape[1] // (2 * experts)
    fits = capacity % 8 == 0 and lax.axis_size("seq") == 2 and routes.shape[1] == 2
    run = fused_on_device if fits else halves_on_device
    return run(tokens, routes, *rest)


def solution(mesh):
    placed = (
        P(("seq", "expert"), None),
        P(("seq", "expert"), None),
        P(("seq", "expert"), None),
        P("expert", None, "seq"),
        P("expert", None, "seq"),
        P("expert", "seq", None),
        P(("seq", "expert"), None),
    )
    return jax.shard_map(
        on_device,
        mesh=mesh,
        in_specs=placed,
        out_specs=(P(("seq", "expert"), None), P(("seq", "expert"), None)),
        check_vma=False,
    )
```
